32 devices in a mesh: gx: 4 (over z), gy: 4 (over x, core), sa: 2 (over y).
Axes of the slice: x: 2, y: 2, z: 4, core: 2. Of those that a mesh axis runs over, the one named last changes fastest.
Arguments:
- field_now: float32 [160, 256, 512], P('sa', 'gy', 'gx'), may hold values from -1.5 to 1.5
- field_before: float32 [160, 256, 512], P('sa', 'gy', 'gx'), may hold values from -1.5 to 1.5
- source: float32 [160, 256, 512], P('sa', 'gy', 'gx'), may hold values from -0.06 to 0.06
- log_fields: float32 [9, 256, 512], P(None, ('gy', 'sa'), 'gx'), may hold values from -0.15 to 0.15
- weights: float32 [1500], replicated, may hold values from 0.0002 to 0.002
- mean_perm: float32 [], replicated, may hold values from 0.5 to 2
- node_index: int32 [1500, 8], replicated, may hold values from 0 to 6
- mode_index: int32 [160, 8], replicated, may hold values from 0 to 3, as said below
Outputs:
- fresh: float32 [160, 256, 512], P('sa', 'gy', 'gx')
- update: float32 [160, 256, 512], P('sa', 'gy', 'gx')
The draws below stay inside these ranges and needn't reach their ends.
Inputs may be any that keep to these rules, and one draw needn't show every extreme that they name: `node_index`: each entry numbers a point of the list in the first step. `mode_index`: the rows are distinct multi-indices of total degree at most 3.
All inputs are finite; a program needn't handle non-finite values.
Results may differ from the reference program's by a relative error of at most 0.0003.
Values sent between devices are 32-bit elements; how exact they have to be, the bound alone decides.
A program may use at most 128 MiB of HBM per device.

```python
import math
import jax
import jax.numpy as jnp
import numpy as np
from jax import lax

G = 8
P_SIZE = 160
Q = 1500
NX = 512
NY = 256


def multi_indices(germ_count, highest):
    listed = [[]]
    for column in range(germ_count):
        listed = [record + [degree] for record in listed for degree in range(highest + 1) if sum(record) + degree <= highest]
    return np.array(listed, dtype=np.int32)


def draw_mode_index(key, part):
    table = jnp.asarray(multi_indices(G, 3))
    shuffled = jax.random.permutation(jax.random.fold_in(key, 17), table.shape[0])
    return table[shuffled[:P_SIZE]]


def plant(result, rng, least, largest):
    longest = result.shape.index(max(result.shape))
    spots = []
    for shift in (0, 1):
        where = [jax.random.randint(jax.random.fold_in(rng, axis), (), 0, length) for axis, length in enumerate(result.shape)]
        where[longest] = (where[longest] + shift) % result.shape[longest]
        spots.append(tuple(where))
    return result.at[spots[0]].set(least).at[spots[1]].set(largest)


def level_of(rng, extent, cuts, low, top_value):
    gain = 1.0
    for position, parts in cuts:
        heights = jax.random.uniform(jax.random.fold_in(jax.random.fold_in(rng, 6), position), (parts,), jnp.float32, low / len(cuts), top_value / len(cuts))
        gain = gain * jnp.repeat(jnp.exp(heights), extent[position] // parts).reshape((-1,) + (1,) * (len(extent) - 1 - position))
    return gain


def scatter_about(key, extent, spread, reach, split=(), kind=jnp.bfloat16):
    values = jax.random.normal(key, extent, jnp.float32) * spread
    if len(split) > 0:
        values = level_of(key, extent, split, -0.22, 0.18) * values
    return jnp.clip(values, min=-reach, max=reach).astype(kind)


def setup_inputs(seed: int = 0) -> dict:
    streams_of = jax.random.split(jax.random.key(seed), 9)
    field_now = scatter_about(streams_of[0], (P_SIZE, NY, NX), 0.1, 1.5, ((0, 2), (1, 4), (2, 4)), jnp.float32)
    field_before = scatter_about(streams_of[1], (P_SIZE, NY, NX), 0.1, 1.5, ((0, 2), (1, 4), (2, 4)), jnp.float32)
    source = scatter_about(streams_of[2], (P_SIZE, NY, NX), 0.01, 0.06, ((0, 2), (1, 4), (2, 4)), jnp.float32)
    log_fields = jnp.clip(jax.random.uniform(streams_of[3], (G + 1, NY, NX), jnp.float32, -0.15, 0.15) * level_of(streams_of[3], (G + 1, NY, NX), ((1, 8), (2, 4)), -0.4, 0.0), -0.15, 0.15)
    weights = jnp.clip(jnp.exp(jax.random.uniform(streams_of[4], (Q,), jnp.float32, math.log(0.0002), math.log(0.002))), 0.0002, 0.002)
    mean_perm = jnp.clip(jnp.exp(jax.random.uniform(streams_of[5], (), jnp.float32, math.log(0.5), math.log(2.0))), 0.5, 2.0)
    node_index = plant(jax.random.randint(streams_of[6], (Q, G), 0, 7), jax.random.fold_in(streams_of[6], 1), 0, 6).astype(jnp.int32)
    mode_index = draw_mode_index(jax.random.fold_in(streams_of[8], 71), 0)
    return {"field_now": field_now, "field_before": field_before, "source": source, "log_fields": log_fields, "weights": weights, "mean_perm": mean_perm, "node_index": node_index, "mode_index": mode_index}


HIGHEST = lax.Precision.HIGHEST
hermite_points = (0.0, -1.7320508075688772, 1.7320508075688772, -1.355626179974266, 1.355626179974266, -2.8569700138728056, 2.8569700138728056)
storage_rate = 0.0004
relax_weight = 1.6
step_length = 0.3

def node_germs(node_index):
    levels = jnp.arange(len(hermite_points), dtype=jnp.int32)
    picked = (node_index[:, :, None] == levels).astype(jnp.float32)
    points = jnp.asarray(hermite_points, dtype=jnp.float32)
    return lax.optimization_barrier(jnp.sum(picked * points, axis=2))

def chaos_basis(node_index, mode_index):
    germ_values = node_germs(node_index)
    square = germ_values * germ_values
    hermite = jnp.stack([jnp.ones_like(germ_values), germ_values, (square - 1.0) / math.sqrt(2.0), (square * germ_values - 3.0 * germ_values) / math.sqrt(6.0)], axis=2)
    degrees = jnp.arange(4, dtype=jnp.int32)
    values = jnp.ones((node_index.shape[0], mode_index.shape[0]), jnp.float32)
    for column in range(mode_index.shape[1]):
        select = (mode_index[:, column][:, None] == degrees).astype(jnp.float32)
        values = values * jnp.dot(hermite[:, column, :], select.T, precision=HIGHEST)
    return (germ_values, values)

def with_mean(germ_values):
    return jnp.concatenate([jnp.ones((germ_values.shape[0], 1), germ_values.dtype), germ_values], axis=1)

def harmonic(later, earlier):
    return 2.0 * later * earlier / (later + earlier)

def apply_operator(values, log_perm):
    conduct = jnp.exp(log_perm)
    across = harmonic(conduct[:, :, 1:], conduct[:, :, :-1]) * (values[:, :, 1:] - values[:, :, :-1])
    along = harmonic(conduct[:, 1:, :], conduct[:, :-1, :]) * (values[:, 1:, :] - values[:, :-1, :])
    across_div = jnp.pad(across, ((0, 0), (0, 0), (0, 1))) - jnp.pad(across, ((0, 0), (0, 0), (1, 0)))
    along_div = jnp.pad(along, ((0, 0), (0, 1), (0, 0))) - jnp.pad(along, ((0, 0), (1, 0), (0, 0)))
    return storage_rate * values - across_div - along_div

def cosine_matrix(length):
    freq = jnp.arange(length, dtype=jnp.int32)[:, None]
    cells = jnp.arange(length, dtype=jnp.int32)[None, :]
    phase = freq * (2 * cells + 1) % (4 * length)
    angle = phase.astype(jnp.float32) * (math.pi / (2 * length))
    factor = jnp.where(freq == 0, math.sqrt(1.0 / length), math.sqrt(2.0 / length))
    return factor * jnp.cos(angle)

def eigen_values(first, count, length):
    freq = (first + jnp.arange(count, dtype=jnp.int32)).astype(jnp.float32)
    return 2.0 - 2.0 * jnp.cos(freq * (math.pi / length))

def reference(field_now, field_before, source, log_fields, weights, mean_perm, node_index, mode_index):
    germ_values, basis = chaos_basis(node_index, mode_index)
    germ_full = with_mean(germ_values)
    node_block = math.gcd(Q, 50)
    blocks = Q // node_block
    node_items = (basis.reshape(blocks, node_block, P_SIZE), germ_full.reshape(blocks, node_block, G + 1), weights.reshape(blocks, node_block))

    def accumulate(running, node_item):
        basis_part, germ_part, weight_part = node_item
        values = jnp.einsum('qp,pyx->qyx', basis_part, field_now, precision=HIGHEST)
        log_perm = jnp.einsum('qg,gyx->qyx', germ_part, log_fields, precision=HIGHEST)
        applied = apply_operator(values, log_perm)
        running = running + jnp.einsum('qp,qyx->pyx', basis_part * weight_part[:, None], applied, precision=HIGHEST)
        return (running, None)
    galerkin, unused = lax.scan(accumulate, jnp.zeros(field_now.shape, jnp.float32), node_items)
    residual = source - galerkin
    rows_matrix = cosine_matrix(NY)
    cols_matrix = cosine_matrix(NX)
    spectral = jnp.einsum('jy,pyx->pjx', rows_matrix, residual, precision=HIGHEST)
    spectral = jnp.einsum('pjx,kx->pjk', spectral, cols_matrix, precision=HIGHEST)
    spectral = spectral / (storage_rate + mean_perm * (eigen_values(0, NY, NY)[:, None] + eigen_values(0, NX, NX)[None, :]))
    spectral = jnp.einsum('pjk,kx->pjx', spectral, cols_matrix, precision=HIGHEST)
    update = jnp.einsum('jy,pjx->pyx', rows_matrix, spectral, precision=HIGHEST)
    fresh = field_before + relax_weight * (field_now - field_before + step_length * update)
    return (fresh, update)
```

```python
import math

import jax
import jax.numpy as jnp
from jax import lax
from jax.experimental import pallas as pl
from jax.experimental.pallas import tpu as pltpu
from jax.sharding import PartitionSpec as P


HIGHEST = lax.Precision.HIGHEST
HIGH = lax.Precision.HIGH
hermite_points = (
    0.0,
    -1.7320508075688772,
    1.7320508075688772,
    -1.355626179974266,
    1.355626179974266,
    -2.8569700138728056,
    2.8569700138728056,
)
storage_rate = 0.0004
relax_weight = 1.6
step_length = 0.3


LANES = 128
NODE_BLOCK = 512
BF16 = jnp.bfloat16


def round_up(value, step):
    return -(-value // step) * step


def split_high(block):
    high = lax.reduce_precision(block, exponent_bits=8, mantissa_bits=7)
    return (high.astype(BF16), (block - high).astype(BF16))


def stacked(block, dim, order, total):
    high, low = split_high(block)
    pieces = [low if kind else high for kind in order]
    joined = jnp.concatenate(pieces, axis=dim)
    widths = [(0, 0)] * joined.ndim
    widths[dim] = (0, total - joined.shape[dim])
    return jnp.pad(joined, widths)


def shifted(last, first, axes):
    count = lax.axis_size(axes)
    forward = [(i, i + 1) for i in range(count - 1)]
    backward = [(target, source) for source, target in forward]
    here = lax.axis_index(axes)
    before = jnp.where(here == 0, first, lax.ppermute(last, axes, forward))
    after = jnp.where(here == count - 1, last, lax.ppermute(first, axes, backward))
    return (before, after)


def dot(left, right):
    return jnp.dot(left, right, preferred_element_type=jnp.float32)


def node_kernel(
    group, basis_ref, germ_ref, weight_ref, field_ref, log_ref, edge_field_ref, edge_log_ref,
    out_ref, edge_ref, value_prev, half_prev, flux_prev,
):
    block, step = pl.program_id(0), pl.program_id(1)
    modes = out_ref.shape[0]

    def at_nodes(field, log_perm):
        return (dot(basis_ref[...], field), jnp.exp(dot(germ_ref[...], log_perm)))

    def flux(later, earlier, half_later, half_earlier):
        return (later - earlier) * pl.reciprocal(half_later + half_earlier)

    def project(applied):
        high = applied.astype(BF16)
        rest = applied - high.astype(jnp.float32)
        middle = rest.astype(BF16)
        low = (rest - middle.astype(jnp.float32)).astype(BF16)
        both = dot(weight_ref[...], high) + dot(weight_ref[...], middle)
        return both[:modes] + both[modes:] + dot(weight_ref[:modes, :], low)

    @pl.when(step == 0)
    def start():
        values, halves = at_nodes(field_ref[:, : 2 * LANES], log_ref[:, : 2 * LANES])
        value_prev[...] = values[:, LANES:]
        half_prev[...] = halves[:, LANES:]
        flux_prev[...] = flux(
            values[:, LANES:], values[:, :LANES], halves[:, LANES:], halves[:, :LANES]
        )
        width = edge_ref.shape[1]
        values, halves = at_nodes(edge_field_ref[...], edge_log_ref[...])
        edge = project(
            flux(values[:, width:], values[:, :width], halves[:, width:], halves[:, :width])
        )

        @pl.when(block == 0)
        def first():
            edge_ref[...] = edge
            out_ref[...] = jnp.zeros_like(out_ref)

        @pl.when(block > 0)
        def later():
            edge_ref[...] += edge

    value, half, flux_up = value_prev[...], half_prev[...], flux_prev[...]
    inside = lax.broadcasted_iota(jnp.int32, value.shape, 1) < LANES - 1
    for pair in range(group // 2):
        ahead = pl.ds(pl.multiple_of((step * group + 2 + 2 * pair) * LANES, LANES), 2 * LANES)
        values, halves = at_nodes(field_ref[:, ahead], log_ref[:, ahead])
        applied = []
        for row in range(2):
            value_next = values[:, row * LANES : (row + 1) * LANES]
            half_next = halves[:, row * LANES : (row + 1) * LANES]
            flux_down = flux(value_next, value, half_next, half)
            across = jnp.where(
                inside,
                flux(
                    pltpu.roll(value, LANES - 1, 1), value, pltpu.roll(half, LANES - 1, 1), half
                ),
                0.0,
            )
            applied.append(
                storage_rate * value - (across - pltpu.roll(across, 1, 1)) - (flux_down - flux_up)
            )
            value, half, flux_up = value_next, half_next, flux_down
        rows = pl.ds(pl.multiple_of((step * group + 2 * pair) * LANES, LANES), 2 * LANES)
        out_ref[:, rows] += project(jnp.concatenate(applied, axis=1))
    value_prev[...] = value
    half_prev[...] = half
    flux_prev[...] = flux_up


def galerkin_product(field, log_fields, germ_full, basis, weights):
    modes, rows, width = field.shape
    nodes = basis.shape[0]
    germs = germ_full.shape[1]
    padded_nodes = round_up(nodes, NODE_BLOCK)
    depth = round_up(3 * modes, LANES)
    log_depth = round_up(3 * (germs + 1), 16)

    both = lambda pick: jnp.concatenate([pick(field), pick(log_fields)], axis=0)
    first_row, last_row = both(lambda a: a[:, 0, :]), both(lambda a: a[:, -1, :])
    first_col, last_col = both(lambda a: a[:, :, 0]), both(lambda a: a[:, :, -1])
    above, below = shifted(last_row, first_row, ("gy", "sa"))
    before, after = shifted(last_col, first_col, "gx")
    edge_width = round_up(2 * rows, LANES)
    fill = jnp.zeros((modes + germs, edge_width - 2 * rows), jnp.float32)
    edges = jnp.concatenate([before, last_col, fill, first_col, after, fill], axis=1)

    def operands(block):
        cells = block.shape[1]
        ones = jnp.ones((1, cells), jnp.float32)
        return (
            stacked(block[:modes], 0, (0, 1, 0), depth),
            stacked(jnp.concatenate([block[modes:], ones]), 0, (0, 1, 0), log_depth),
        )

    def tall(block, lo, hi):
        return jnp.concatenate(
            [above[lo:hi], block.reshape(hi - lo, rows * width), below[lo:hi]], axis=1
        )

    cells = jnp.concatenate(
        [tall(field, 0, modes), tall(log_fields, modes, modes + germs)], axis=0
    )
    field_op, log_op = operands(cells)
    edge_field_op, edge_log_op = operands(edges)
    extend = lambda a: jnp.pad(a, ((0, padded_nodes - nodes), (0, 0)))
    basis_op = stacked(extend(basis), 1, (0, 0, 1), depth)
    log_half = jnp.full((nodes, 1), -math.log(2.0), jnp.float32)
    germ_op = stacked(
        extend(jnp.concatenate([-germ_full, log_half], axis=1)), 1, (0, 0, 1), log_depth
    )
    weight_op = stacked(extend(basis * weights[:, None]).T, 0, (0, 1), 2 * modes)

    group = math.gcd(rows, 8)
    whole = lambda a: pl.BlockSpec(a.shape, lambda q, g: (0, 0))
    carry = pltpu.VMEM((NODE_BLOCK, LANES), jnp.float32)
    galerkin, edge = pl.pallas_call(
        lambda *refs: node_kernel(group, *refs),
        grid=(padded_nodes // NODE_BLOCK, rows // group),
        in_specs=[
            pl.BlockSpec((NODE_BLOCK, depth), lambda q, g: (q, 0)),
            pl.BlockSpec((NODE_BLOCK, log_depth), lambda q, g: (q, 0)),
            pl.BlockSpec((2 * modes, NODE_BLOCK), lambda q, g: (0, q)),
            whole(field_op),
            whole(log_op),
            whole(edge_field_op),
            whole(edge_log_op),
        ],
        out_specs=[
            pl.BlockSpec((modes, rows * width), lambda q, g: (0, 0)),
            pl.BlockSpec((modes, edge_width), lambda q, g: (0, 0)),
        ],
        out_shape=[
            jax.ShapeDtypeStruct((modes, rows * width), jnp.float32),
            jax.ShapeDtypeStruct((modes, edge_width), jnp.float32),
        ],
        scratch_shapes=[carry, carry, carry],
        compiler_params=pltpu.CompilerParams(
            dimension_semantics=("arbitrary", "arbitrary"), vmem_limit_bytes=56 * 1024 * 1024
        ),
    )(basis_op, germ_op, weight_op, field_op, log_op, edge_field_op, edge_log_op)
    place = jnp.arange(width, dtype=jnp.int32)
    return (
        galerkin.reshape(modes, rows, width)
        + jnp.where(place == 0, edge[:, :rows, None], 0.0)
        - jnp.where(place == width - 1, edge[:, rows : 2 * rows, None], 0.0)
    )


def node_germs(node_index):
    levels = jnp.arange(len(hermite_points), dtype=jnp.int32)
    picked = (node_index[:, :, None] == levels).astype(jnp.float32)
    points = jnp.asarray(hermite_points, dtype=jnp.float32)
    return jnp.sum(picked * points, axis=2)


def chaos_basis(node_index, mode_index):
    germ_values = node_germs(node_index)
    square = germ_values * germ_values
    hermite = jnp.stack(
        [
            jnp.ones_like(germ_values),
            germ_values,
            (square - 1.0) / math.sqrt(2.0),
            (square * germ_values - 3.0 * germ_values) / math.sqrt(6.0),
        ],
        axis=2,
    )
    degrees = jnp.arange(4, dtype=jnp.int32)
    values = jnp.ones((node_index.shape[0], mode_index.shape[0]), jnp.float32)
    for column in range(mode_index.shape[1]):
        select = (mode_index[:, column][:, None] == degrees).astype(jnp.float32)
        values = values * jnp.dot(hermite[:, column, :], select.T, precision=HIGHEST)
    return (germ_values, values)


def with_mean(germ_values):
    return jnp.concatenate(
        [jnp.ones((germ_values.shape[0], 1), germ_values.dtype), germ_values], axis=1
    )


def cosine_matrix(length):
    freq = jnp.arange(length, dtype=jnp.int32)[:, None]
    cells = jnp.arange(length, dtype=jnp.int32)[None, :]
    phase = freq * (2 * cells + 1) % (4 * length)
    angle = phase.astype(jnp.float32) * (math.pi / (2 * length))
    factor = jnp.where(freq == 0, math.sqrt(1.0 / length), math.sqrt(2.0 / length))
    return factor * jnp.cos(angle)


def eigen_values(first, count, length):
    freq = (first + jnp.arange(count, dtype=jnp.int32)).astype(jnp.float32)
    return 2.0 - 2.0 * jnp.cos(freq * (math.pi / length))


def on_device(
    field_now, field_before, source, log_fields, weights, mean_perm, node_index, mode_index
):
    germ_values, basis = chaos_basis(node_index, mode_index)
    germ_full = with_mean(germ_values)
    moved_field = lax.all_to_all(field_now, "sa", split_axis=1, concat_axis=0, tiled=True)
    source_moved = lax.all_to_all(source, "sa", split_axis=1, concat_axis=0, tiled=True)
    galerkin = galerkin_product(moved_field, log_fields, germ_full, basis, weights)
    return fresh_update(field_now, field_before, source_moved - galerkin, mean_perm)


def fresh_update(field_now, field_before, residual, mean_perm):
    gy, sa, gx = (lax.axis_size(axis) for axis in ("gy", "sa", "gx"))
    modes, rows, width = residual.shape
    part = modes // (gy * sa)
    residual = residual.reshape(sa, gy, part, rows, width).transpose(1, 0, 2, 3, 4)
    pencil = lax.all_to_all(
        residual.reshape(modes, rows, width), ("gy", "sa"), split_axis=0, concat_axis=1, tiled=True
    )
    full_rows = pencil.shape[1]
    rows_matrix = cosine_matrix(full_rows)
    cols_matrix = cosine_matrix(width)
    ends = jnp.stack([cols_matrix[:, 0], cols_matrix[:, -1]])
    row_eigen = eigen_values(0, full_rows, full_rows)
    col_eigen = eigen_values(0, width, width)
    inverse = 1.0 / (storage_rate + mean_perm * (row_eigen[:, None] + col_eigen[None, :]))
    spectral = jnp.einsum("jy,myx->mjx", rows_matrix, pencil, precision=HIGHEST)
    spectral = jnp.einsum("mjx,kx->mjk", spectral, cols_matrix, precision=HIGHEST)
    if gx > 1:
        own = jnp.einsum("mjk,ck->cmj", spectral * inverse, ends, precision=HIGHEST)
        every = lax.all_to_all(
            jnp.broadcast_to(own, (gx,) + own.shape), "gx", split_axis=0, concat_axis=0, tiled=True
        ).reshape((gx,) + own.shape)
        jump = every[1:, 0] - every[:-1, 1]
        same = jnp.sum(inverse * (ends[0] * ends[0]), axis=1)
        cross = jnp.sum(inverse * (ends[0] * ends[1]), axis=1)
        number = jnp.arange(1, gx, dtype=jnp.int32)
        sines = jnp.sin(
            ((number[:, None] * number[None, :]) % (2 * gx)).astype(jnp.float32) * (math.pi / gx)
        )
        turns = jnp.cos(number.astype(jnp.float32) * (math.pi / gx))
        shrink = 1.0 / (
            1.0 / mean_perm + 2.0 * same[None, :] - 2.0 * cross[None, :] * turns[:, None]
        )
        to_flux = (2.0 / gx) * jnp.sum(
            sines[:, :, None, None] * sines[:, None, :, None]
            * shrink[:, None, None, :],
            axis=0,
        )
        to_flux = jnp.pad(to_flux, ((1, 1), (0, 0), (0, 0)))
        here = lax.axis_index("gx")
        left = lax.dynamic_index_in_dim(to_flux, here, 0, keepdims=False)
        right = lax.dynamic_index_in_dim(to_flux, here + 1, 0, keepdims=False)
        flux_left = jnp.sum(left[:, None, :] * jump, axis=0)
        flux_right = jnp.sum(right[:, None, :] * jump, axis=0)
        spectral = spectral + (
            flux_right[:, :, None] * ends[1] - flux_left[:, :, None] * ends[0]
        )
    spectral = spectral * inverse
    columns = jnp.einsum("mjk,kx->mjx", spectral, cols_matrix, precision=HIGH)
    update_cols = jnp.einsum("jy,mjx->myx", rows_matrix, columns, precision=HIGH)
    update = lax.all_to_all(update_cols, "gy", split_axis=1, concat_axis=0, tiled=True)
    fresh = field_before + relax_weight * (field_now - field_before + step_length * update)
    return (fresh, update)


def solution(mesh):
    return jax.shard_map(
        on_device,
        mesh=mesh,
        in_specs=(
            P("sa", "gy", "gx"),
            P("sa", "gy", "gx"),
            P("sa", "gy", "gx"),
            P(None, ("gy", "sa"), "gx"),
            P(),
            P(),
            P(),
            P(),
        ),
        out_specs=(P("sa", "gy", "gx"), P("sa", "gy", "gx")),
        check_vma=False,
    )
```
